1024 devices in a mesh: lon: 64 (over y_lo, x, core), head: 16 (over y_hi, z).
Axes of the slice: x: 8, y: 8 (y_hi: 2, y_lo: 4; y = y_hi * 4 + y_lo), z: 8, core: 2. Of those that a mesh axis runs over, the one named last changes fastest.
Arguments:
- activations: bfloat16 [131072, 1024], P('lon')
- qkv_weight: bfloat16 [1024, 3072], P(None, 'head'), may hold values from -0.1875 to 0.1875
- attn_grad: bfloat16 [131072, 1024], P('lon', 'head'), may hold values from -6 to 6
- pos_bias: float32 [16, 128, 128], P('head'), may hold values from -4 to 4
- key_counts: int32 [1024], P('lon'), may hold values from 32 to 128, as said below
Outputs:
- input_grad: bfloat16 [131072, 1024], P(('lon', 'head'))
- weight_grad: float32 [1024, 3072], P(None, 'head')
The draws below stay inside these ranges and needn't reach their ends.
Inputs may be any that keep to these rules, and one draw needn't show every extreme that they name: key_counts[g] is the number of valid keys of shifted window g; windows of window row 0 and of the last window row may hold fewer than 128, all others hold 128.
All inputs are finite; a program needn't handle non-finite values.
Results may differ from the reference program's by a relative error of at most 0.019.
The reference program's roundings to bfloat16 on the way (of `projected` and `grad_proj`) count: a program that leaves them out, or rounds other values in their place, can miss the bound.
Values may be sent and summed in bfloat16 or wider, within the bound.
A program may use at most 64 MiB of HBM per device.

```python
import math
import jax
import jax.numpy as jnp
from jax import lax

D = 1024
HEADS = 16
HEAD_DIM = 64
WIN = 128
WIN_ROWS = 8
WIN_COLS = 2
TOKENS = 131072
WINDOWS = 1024
N_LON = 64
N_HEAD = 16


def draw_activations(key, part):
    first_key, second_key = jax.random.split(jax.random.fold_in(key, 11))
    values = jax.random.normal(first_key, (TOKENS, D), jnp.float32)
    scales = jnp.exp(jax.random.uniform(second_key, (TOKENS, 1), jnp.float32, math.log(0.5), math.log(2.0)))
    return jnp.clip(values * scales, -12.0, 12.0).astype(jnp.bfloat16)


def draw_key_counts(key, part):
    index = jnp.arange(WINDOWS, dtype=jnp.int32)
    row_index = index // WIN_COLS % WIN_ROWS
    polar = (row_index == 0) | (row_index == WIN_ROWS - 1)
    drawn = jax.random.randint(jax.random.fold_in(key, 23), (WINDOWS,), WIN // 4, WIN + 1, dtype=jnp.int32)
    return jnp.where(polar, drawn, WIN).astype(jnp.int32)


def shard_levels(key, shape, pieces, least, high):
    loudness = 1.0
    for axis_at, parts in pieces:
        steps = jax.random.uniform(jax.random.fold_in(jax.random.fold_in(key, 6), axis_at), (parts,), jnp.float32, least / len(pieces), high / len(pieces))
        loudness = loudness * jnp.repeat(jnp.exp(steps), shape[axis_at] // parts).reshape((-1,) + (1,) * (len(shape) - 1 - axis_at))
    return loudness


def normal_values(key, extent, spread, limit, shards=(), held_as=jnp.bfloat16):
    values = spread * jax.random.normal(key, extent, jnp.float32)
    if shards:
        values = values * shard_levels(key, extent, shards, -0.22, 0.18)
    return jnp.clip(values, -limit, limit).astype(held_as)


def setup_inputs(seed: int = 0) -> dict:
    keys = jax.random.split(jax.random.key(seed), 6)
    activations = draw_activations(jax.random.fold_in(keys[5], 71), 0)
    qkv_weight = normal_values(keys[1], (D, HEADS * 3 * HEAD_DIM), D ** -0.5, 0.1875, ((1, 16),))
    attn_grad = normal_values(keys[2], (TOKENS, HEADS * HEAD_DIM), 1.0, 6.0, ((0, 64), (1, 16)))
    pos_bias = normal_values(keys[3], (HEADS, WIN, WIN), 1.0, 4.0, ((0, 16),), jnp.float32)
    key_counts = draw_key_counts(jax.random.fold_in(keys[5], 71), 0)
    return dict(activations=activations, qkv_weight=qkv_weight, attn_grad=attn_grad, pos_bias=pos_bias, key_counts=key_counts)


def assemble(block_grid, far_rows):
    half_len = block_grid.shape[3]
    first_part = block_grid[:, :, 1]
    second_part = jnp.concatenate([block_grid[:, 1:, 0], far_rows[:, None]], axis=1)
    return jnp.concatenate([first_part, second_part], axis=2)

def window_grads(proj_win, delta_win, pos_bias, valid_count):
    scale_factor = 1.0 / math.sqrt(proj_win.shape[-1])
    queries = proj_win[:, :, :, 0].astype(jnp.float32)
    keys_part = proj_win[:, :, :, 1].astype(jnp.float32)
    values_part = proj_win[:, :, :, 2].astype(jnp.float32)
    delta_full = delta_win.astype(jnp.float32)
    scores = jnp.einsum('nqhe,nkhe->nhqk', queries, keys_part) * scale_factor + pos_bias[None].astype(jnp.float32)
    positions = jnp.arange(proj_win.shape[1], dtype=jnp.int32)
    valid_keys = positions[None, :] < valid_count[:, None]
    scores = jnp.where(valid_keys[:, None, None, :], scores, -jnp.inf)
    row_max = lax.optimization_barrier(jnp.max(scores, axis=-1, keepdims=True))
    weights = jnp.exp(scores - row_max)
    probs = weights / lax.optimization_barrier(jnp.sum(weights, axis=-1, keepdims=True))
    grad_probs = jnp.einsum('nqhe,nkhe->nhqk', delta_full, values_part)
    grad_scores = probs * (grad_probs - lax.optimization_barrier(jnp.sum(probs * grad_probs, axis=-1, keepdims=True)))
    probs_low = probs.astype(jnp.bfloat16).astype(jnp.float32)
    grads_low = grad_scores.astype(jnp.bfloat16).astype(jnp.float32)
    grad_values = jnp.einsum('nhqk,nqhe->nkhe', probs_low, delta_full)
    grad_queries = jnp.einsum('nhqk,nkhe->nqhe', grads_low, keys_part) * scale_factor
    grad_keys = jnp.einsum('nhqk,nqhe->nkhe', grads_low, queries) * scale_factor
    return jnp.stack([grad_queries, grad_keys, grad_values], axis=3).astype(jnp.bfloat16)

def reference(activations, qkv_weight, attn_grad, pos_bias, key_counts):
    half_len = WIN // 2
    width_all = HEADS * 3 * HEAD_DIM
    projected = jnp.dot(activations, qkv_weight, preferred_element_type=jnp.float32).astype(jnp.bfloat16)
    proj_grid = projected.reshape(N_LON, WIN_ROWS, WIN_COLS, 2, half_len, width_all)
    delta_grid = attn_grad.reshape(N_LON, WIN_ROWS, WIN_COLS, 2, half_len, HEADS * HEAD_DIM)
    far_proj = jnp.roll(proj_grid[:, :, 0, 0], -1, axis=0)
    far_delta = jnp.roll(delta_grid[:, :, 0, 0], -1, axis=0)
    band_counts = key_counts.reshape(N_LON, WIN_ROWS * WIN_COLS)

    def one_band(items):
        block_grid, far_rows, delta_block, delta_far, valid_count = items
        proj_win = assemble(block_grid, far_rows).reshape(WIN_ROWS * WIN_COLS, WIN, HEADS, 3, HEAD_DIM)
        delta_win = assemble(delta_block, delta_far).reshape(WIN_ROWS * WIN_COLS, WIN, HEADS, HEAD_DIM)
        result = window_grads(proj_win, delta_win, pos_bias, valid_count)
        return result.reshape(WIN_ROWS, WIN_COLS, WIN, width_all)
    gradients = lax.map(one_band, (proj_grid, far_proj, delta_grid, far_delta, band_counts))
    leading = gradients[:, :, :, :half_len]
    trailing = gradients[:, :, :, half_len:]
    returned = jnp.roll(trailing[:, :, WIN_COLS - 1], 1, axis=0)
    first_halves = jnp.concatenate([returned[:, :, None], trailing[:, :, :WIN_COLS - 1]], axis=2)
    grad_proj = jnp.stack([first_halves, leading], axis=3).reshape(TOKENS, width_all)
    group_width = width_all // N_HEAD
    input_grad = jnp.zeros((TOKENS, D), jnp.float32)
    for group_index in range(N_HEAD):
        low_col = group_index * group_width
        partial_grad = lax.dot_general(grad_proj[:, low_col:low_col + group_width], qkv_weight[:, low_col:low_col + group_width], (((1,), (1,)), ((), ())), preferred_element_type=jnp.float32)
        input_grad = input_grad + lax.optimization_barrier(partial_grad.astype(jnp.bfloat16)).astype(jnp.float32)
    weight_grad = lax.dot_general(activations, grad_proj, (((0,), (0,)), ((), ())), preferred_element_type=jnp.float32) / math.sqrt(TOKENS)
    return (input_grad.astype(jnp.bfloat16), weight_grad)
```

```python
import math

import jax
import jax.numpy as jnp
from jax import lax
from jax.experimental import pallas as pl
from jax.experimental.pallas import tpu as pltpu
from jax.sharding import PartitionSpec as P

MESH = pl.DeviceIdType.MESH
F32 = jnp.float32
BF16 = jnp.bfloat16
D = 1024
HEAD_DIM = 64
WIN = 128
ROWS = 8
N_LON = 64
TOKENS = 131072
SCALE = 1.0 / math.sqrt(HEAD_DIM)
WG_SCALE = 1.0 / math.sqrt(TOKENS)
NT = (((1,), (1,)), ((), ()))
TN = (((0,), (0,)), ((), ()))
NN = (((1,), (0,)), ((), ()))


def dot(a, b, dims):
    return lax.dot_general(a, b, dims, preferred_element_type=F32)


def kernel(
    x_ref, wt_ref, a_ref, bias_ref, cnt_ref, out_ref, wg_ref,
    xs, ah, proj, biast, gpf, gps, gat, wgat, lhs, acc, ysend, yrecv,
    wacc, s_s, r_s, t_x, s_x, r_x, t_y, s_y, r_y, og,
    load_sem, own_sem, halo_s, halo_r, ahalo_s, ahalo_r, piece_s, piece_r,
    up_s, up_r, down_s, down_r, sib_s, sib_r, y_s, y_r,
    rss_s, rss_r, rsx_s, rsx_r, rsy_s, rsy_r, agy_s, agy_r, agx_s, agx_r, ags_s, ags_r,
):
    me_l = lax.axis_index("lon")
    me_h = lax.axis_index("head")
    yh, z = lax.div(me_h, 8), lax.rem(me_h, 8)
    core = lax.rem(me_l, 2)
    x = lax.rem(lax.div(me_l, 2), 8)
    yl = lax.div(me_l, 16)
    after = lax.rem(me_l + 1, N_LON)
    before = lax.rem(me_l + N_LON - 1, N_LON)
    sibling = me_l + 1 - 2 * core

    def remote(src, dst, send, recv, device):
        return pltpu.make_async_remote_copy(
            src_ref=src, dst_ref=dst, send_sem=send, recv_sem=recv, device_id=device, device_id_type=MESH
        )

    def z_peer(zz):
        return (me_l, yh * 8 + zz)

    def x_peer(i):
        return ((yl * 8 + lax.rem(x + i, 8)) * 2 + core, me_h)

    def y_peer(i):
        return ((lax.rem(yl + i, 4) * 8 + x) * 2 + core, me_h)

    partner = (me_l, (1 - yh) * 8 + z)

    load0 = pltpu.make_async_copy(x_ref.at[:, pl.ds(64, 128)], xs.at[:, pl.ds(0, 128)], load_sem.at[0])
    load1 = pltpu.make_async_copy(x_ref.at[:, pl.ds(192, 64)], xs.at[:, pl.ds(128, 64)], load_sem.at[1])
    load0.start()
    load1.start()
    own_w = pltpu.make_async_copy(wt_ref, wgat.at[z], own_sem)
    own_w.start()

    barrier = pltpu.get_barrier_semaphore()
    peers = [z_peer(lax.rem(z + i, 8)) for i in range(1, 8)]
    peers += [(near, yh * 8 + zz) for near in (after, before) for zz in range(8)]
    peers += [x_peer(i) for i in range(1, 8)] + [y_peer(i) for i in range(1, 4)] + [partner]
    for peer in peers:
        pl.semaphore_signal(barrier, inc=1, device_id=peer, device_id_type=MESH)
    pl.semaphore_wait(barrier, len(peers))

    def group(i):
        return 4 * lax.rem(1 - yh + i, 2)

    halo = [
        remote(
            x_ref.at[pl.ds(group(i), 4), pl.ds(0, 64)], xs.at[pl.ds(group(i), 4), pl.ds(192, 64)],
            halo_s.at[i], halo_r.at[i], (before, me_h),
        )
        for i in range(2)
    ]
    a_halo = remote(a_ref.at[:, pl.ds(0, 64)], ah, ahalo_s, ahalo_r, (before, me_h))
    a_halo.start()
    halo[0].start()
    halo[1].start()

    def up(k):
        slot = lax.rem(z + 8 - k, 8)
        src = wt_ref.at[core] if k == 0 else wgat.at[slot, core]
        return remote(src, wgat.at[slot, core], up_s.at[k], up_r.at[k], z_peer(lax.rem(z + 1, 8)))

    def down(k):
        slot = lax.rem(z + k, 8)
        src = wt_ref.at[core] if k == 0 else wgat.at[slot, core]
        return remote(src, wgat.at[slot, core], down_s.at[k], down_r.at[k], z_peer(lax.rem(z + 7, 8)))

    def to_sibling(n, slot):
        return remote(wgat.at[slot, core], wgat.at[slot, core], sib_s.at[n], sib_r.at[n], (sibling, me_h))

    up(0).start()
    down(0).start()

    def pump(k):
        up(k).wait_recv()
        if k < 3:
            up(k + 1).start()
        to_sibling(k, lax.rem(z + 7 - k, 8)).start()
        if k < 3:
            down(k).wait_recv()
            if k < 2:
                down(k + 1).start()
            to_sibling(4 + k, lax.rem(z + 1 + k, 8)).start()

    biast[...] = bias_ref[...].T

    def project(c, base):
        w = wt_ref[...].reshape(192, D)
        for j in range(0, 4, 2):
            rows = xs[pl.ds(base + j, 2), c * 128:(c + 1) * 128, :].reshape(256, D)
            proj[pl.ds(base + j, 2), c * 128:(c + 1) * 128, :] = (
                dot(rows, w, NT).astype(BF16).reshape(2, 128, 192)
            )

    def window(c, r):
        p = proj[r, c * 128:(c + 1) * 128, :]
        q, k, v = p[:, 0:64], p[:, 64:128], p[:, 128:192]
        if c == 0:
            a = a_ref[r, 64:192, :]
        else:
            a = jnp.concatenate([a_ref[r, 192:256, :], ah[r]], axis=0)
        scores = dot(k, q, NT) * SCALE + biast[...]
        position = lax.broadcasted_iota(jnp.int32, (WIN, WIN), 0)
        scores = jnp.where(position < cnt_ref[2 * r + c], scores, -jnp.inf)
        top = jnp.max(scores, axis=0, keepdims=True)
        weights = jnp.exp(scores - top)
        probs = weights / jnp.sum(weights, axis=0, keepdims=True)
        grad_probs = dot(v, a, NT)
        grads = probs * (grad_probs - jnp.sum(probs * grad_probs, axis=0, keepdims=True))
        probs_low = probs.astype(BF16)
        grads_low = grads.astype(BF16)
        dv = dot(probs_low, a, NN).astype(BF16)
        dk = dot(grads_low, q, NN) * SCALE
        dq = dot(grads_low, k, TN) * SCALE
        qk = jnp.concatenate([dq, dk], axis=1).astype(BF16)
        gpf[r, c * 128:(c + 1) * 128, 0:128] = qk
        gpf[r, c * 128:(c + 1) * 128, 128:192] = dv
        for half in range(2):
            lo = half * 64
            gps[r, 2 * c + half, 0:64, :] = qk[lo:lo + 64]
            gps[r, 2 * c + half, 64:96, :] = jnp.concatenate([dv[lo:lo + 32], dv[lo + 32:lo + 64]], axis=1)

    def piece(r, n):
        block = lax.rem(2 * r + (1 if n in (1, 2) else 0), 8)
        half = 1 if n in (0, 2) else 0
        src = gps.at[r, n]
        dst = gat.at[lax.div(r, 4), half, z]
        recv = piece_r.at[lax.div(r, 4), half, z]
        lon = after if n == 3 else me_l
        far = remote(src, dst, piece_s.at[r, n], recv, (lon, yh * 8 + block))
        near = None if n == 3 else pltpu.make_async_copy(src, dst, recv)
        return block, far, near

    def send_piece(r, n):
        block, far, near = piece(r, n)
        if near is None:
            far.start()
            return

        @pl.when(block == z)
        def _():
            near.start()

        @pl.when(block != z)
        def _():
            far.start()

    def attend(c, base):
        for j in range(4):
            window(c, base + j)
        for j in range(4):
            for half in range(2):
                send_piece(base + j, 2 * c + half)

    def weight_part(c):
        g = gpf[:, c * 128:(c + 1) * 128, :].reshape(1024, 192)
        for n in range(4):
            rows = xs[:, c * 128:(c + 1) * 128, n * 256:(n + 1) * 256].reshape(1024, 256)
            part = dot(g, rows, TN).reshape(2, 96, 256)
            if c == 0:
                wacc[:, :, n * 256:(n + 1) * 256] = part
            else:
                wacc[:, :, n * 256:(n + 1) * 256] += part

    load0.wait()
    for i in range(2):
        project(0, group(i))
        attend(0, group(i))
    weight_part(0)
    pump(0)
    load1.wait()
    a_halo.wait_recv()
    for i in range(2):
        halo[i].wait_recv()
        project(1, group(i))
        attend(1, group(i))
        if i == 0:
            pump(1)
    weight_part(1)

    s_s[...] = wacc[1 - core].astype(BF16)
    rss = remote(s_s, r_s, rss_s, rss_r, (sibling, me_h))
    rss.start()
    pump(2)
    rss.wait_recv()
    for i in range(8):
        cols = slice(i * 128, (i + 1) * 128)
        chunk = wacc[core, :, cols] + r_s[:, cols].astype(F32)
        t_x[i] = chunk
        s_x[i] = chunk.astype(BF16)
    rsx = [
        remote(s_x.at[lax.rem(x + i, 8)], r_x.at[i - 1], rsx_s.at[i - 1], rsx_r.at[i - 1], x_peer(i))
        for i in range(1, 8)
    ]
    for copy in rsx:
        copy.start()
    pump(3)
    for copy in rsx:
        copy.wait_recv()
    total = t_x[x]
    for i in range(7):
        total += r_x[i].astype(F32)
    for i in range(4):
        t_y[i] = total[i * 24:(i + 1) * 24]
        s_y[i] = total[i * 24:(i + 1) * 24].astype(BF16)
    rsy = [
        remote(s_y.at[lax.rem(yl + i, 4)], r_y.at[i - 1], rsy_s.at[i - 1], rsy_r.at[i - 1], y_peer(i))
        for i in range(1, 4)
    ]
    for copy in rsy:
        copy.start()

    own_w.wait()
    for n in range(7):
        to_sibling(n, 0).wait_recv()

    def gather(q):
        for half in range(2):
            for s in range(8):
                pltpu.make_async_copy(gps.at[0, 0], gat.at[q, half, s], piece_r.at[q, half, s]).wait()
        for s in range(8):
            for half in range(2):
                lo = half * 64
                lhs[s, lo:lo + 64, 0:128] = gat[q, half, s, 0:64, :]
                lhs[s, lo:lo + 32, 128:192] = gat[q, half, s, 64:96, 0:64]
                lhs[s, lo + 32:lo + 64, 128:192] = gat[q, half, s, 64:96, 64:128]

    def multiply(n):
        cols = slice(n * 256, (n + 1) * 256)
        total = None
        for s in range(8):
            part = dot(lhs[s], wgat[s, :, :, cols].reshape(192, 256), NN)
            total = part if total is None else total + part
        return total

    gather(1 - yh)
    for n in range(4):
        ysend[:, n * 256:(n + 1) * 256] = multiply(n).astype(BF16)
    exchange = remote(ysend, yrecv, y_s, y_r, partner)
    exchange.start()

    for copy in rsy:
        copy.wait_recv()
    total = t_y[yl]
    for i in range(3):
        total += r_y[i].astype(F32)
    og[core, x, yl] = (total * WG_SCALE).astype(BF16)
    mine = og.at[core, x, yl]
    agy = [remote(mine, mine, agy_s.at[i - 1], agy_r.at[i - 1], y_peer(i)) for i in range(1, 4)]
    for copy in agy:
        copy.start()

    gather(yh)
    for n in range(4):
        acc[:, n * 256:(n + 1) * 256] = multiply(n)

    for copy in agy:
        copy.wait_recv()
    mine_x = og.at[core, x]
    agx = [remote(mine_x, mine_x, agx_s.at[i - 1], agx_r.at[i - 1], x_peer(i)) for i in range(1, 8)]
    for copy in agx:
        copy.start()
    for copy in agx:
        copy.wait_recv()
    ags = remote(og.at[core], og.at[core], ags_s, ags_r, (sibling, me_h))
    ags.start()

    exchange.wait_recv()
    out_ref[...] = (acc[...] + yrecv[...].astype(F32)).astype(BF16)
    ags.wait_recv()
    for c in range(2):
        for i in range(8):
            for j in range(4):
                lo = c * 96 + j * 24
                wg_ref[lo:lo + 24, i * 128:(i + 1) * 128] = og[c, i, j].astype(F32)

    for k in range(4):
        up(k).wait_send()
    for k in range(3):
        down(k).wait_send()
    for n in range(7):
        to_sibling(n, 0).wait_send()
    a_halo.wait_send()
    for copy in halo:
        copy.wait_send()

    @pl.loop(0, ROWS)
    def _(r):
        for n in range(4):
            block, far, near = piece(r, n)
            if near is None:
                far.wait_send()
            else:

                @pl.when(block != z)
                def _():
                    far.wait_send()

    for copy in [rss, exchange, ags] + rsx + rsy + agy + agx:
        copy.wait_send()


def shards(activations, qkv_weight, attn_grad, pos_bias, key_counts):
    dma = pltpu.SemaphoreType.DMA
    vmem = pl.BlockSpec(memory_space=pltpu.VMEM)
    out, wg = pl.pallas_call(
        kernel,
        out_shape=(
            jax.ShapeDtypeStruct((128, D), BF16),
            jax.ShapeDtypeStruct((192, D), F32),
        ),
        in_specs=[
            pl.BlockSpec(memory_space=pl.ANY), vmem, vmem, vmem, pl.BlockSpec(memory_space=pltpu.SMEM),
        ],
        out_specs=(vmem, vmem),
        scratch_shapes=[
            pltpu.VMEM((8, 256, D), BF16),
            pltpu.VMEM((8, 64, 64), BF16),
            pltpu.VMEM((8, 256, 192), BF16),
            pltpu.VMEM((WIN, WIN), F32),
            pltpu.VMEM((8, 256, 192), BF16),
            pltpu.VMEM((8, 4, 96, 128), BF16),
            pltpu.VMEM((2, 2, 8, 96, 128), BF16),
            pltpu.VMEM((8, 2, 96, D), BF16),
            pltpu.VMEM((8, 128, 192), BF16),
            pltpu.VMEM((128, D), F32),
            pltpu.VMEM((128, D), BF16),
            pltpu.VMEM((128, D), BF16),
            pltpu.VMEM((2, 96, D), F32),
            pltpu.VMEM((96, D), BF16),
            pltpu.VMEM((96, D), BF16),
            pltpu.VMEM((8, 96, 128), F32),
            pltpu.VMEM((8, 96, 128), BF16),
            pltpu.VMEM((7, 96, 128), BF16),
            pltpu.VMEM((4, 24, 128), F32),
            pltpu.VMEM((4, 24, 128), BF16),
            pltpu.VMEM((3, 24, 128), BF16),
            pltpu.VMEM((2, 8, 4, 24, 128), BF16),
            dma((2,)), dma,
            dma((2,)), dma((2,)), dma, dma,
            dma((8, 4)), dma((2, 2, 8)),
            dma((4,)), dma((4,)), dma((3,)), dma((3,)),
            dma((7,)), dma((7,)), dma, dma,
            dma, dma, dma((7,)), dma((7,)), dma((3,)), dma((3,)),
            dma((3,)), dma((3,)), dma((7,)), dma((7,)), dma, dma,
        ],
        compiler_params=pltpu.CompilerParams(
            collective_id=0, has_side_effects=True, vmem_limit_bytes=48 * 1024 * 1024
        ),
    )(
        activations.reshape(ROWS, 256, D),
        qkv_weight.T.reshape(2, 96, D),
        attn_grad.reshape(ROWS, 256, HEAD_DIM),
        pos_bias[0],
        key_counts,
    )
    return out, wg.T


def solution(mesh):
    placed = (P("lon", None), P(None, "head"), P("lon", "head"), P("head", None, None), P("lon"))
    return jax.shard_map(
        shards,
        mesh=mesh,
        in_specs=placed,
        out_specs=(P(("lon", "head"), None), P(None, "head")),
        check_vma=False,
    )
```

```python
import math

import jax
import jax.numpy as jnp
from jax import lax
from jax.experimental import pallas as pl
from jax.experimental.pallas import tpu as pltpu
from jax.sharding import PartitionSpec as P

MESH = pl.DeviceIdType.MESH
F32 = jnp.float32
BF16 = jnp.bfloat16
D = 1024
HEAD_DIM = 64
WIN = 128
ROWS = 8
N_LON = 64
TOKENS = 131072
SCALE = 1.0 / math.sqrt(HEAD_DIM)
WG_SCALE = 1.0 / math.sqrt(TOKENS)
NT = (((1,), (1,)), ((), ()))
TN = (((0,), (0,)), ((), ()))
NN = (((1,), (0,)), ((), ()))


def dot(a, b, dims):
    return lax.dot_general(a, b, dims, preferred_element_type=F32)


def kernel(
    x_ref, w_ref, at_ref, b_ref, c_ref, out_ref, wg_ref,
    xs, wt_ref, at, a_ref, bias_ref, cnt_ref, ah, proj, biast, gpf, gps, gat, wgat, lhs, acc, ysend, yrecv,
    wacc, s_s, r_s, t_x, s_x, r_x, r_y, og,
    load_sem, own_sem, halo_s, halo_r, ahalo_s, ahalo_r, piece_s, piece_r,
    up_s, up_r, down_s, down_r, pair_s, pair_r, sib_s, sib_r, y_s, y_r,
    rss_s, rss_r, rsx_s, rsx_r, rsy_s, rsy_r, agx_s, agx_r, ags_s, ags_r,
):
    me_l = lax.axis_index("lon")
    me_h = lax.axis_index("head")
    yh, z = lax.div(me_h, 8), lax.rem(me_h, 8)
    core = lax.rem(me_l, 2)
    x = lax.rem(lax.div(me_l, 2), 8)
    yl = lax.div(me_l, 16)
    after = lax.rem(me_l + 1, N_LON)
    before = lax.rem(me_l + N_LON - 1, N_LON)
    sibling = me_l + 1 - 2 * core
    odd = lax.rem(yl, 2)
    mine, theirs = odd * 2 + core, (1 - odd) * 2 + core
    pair = (me_l + 16 - 32 * odd, me_h)

    def remote(src, dst, send, recv, device):
        return pltpu.make_async_remote_copy(
            src_ref=src, dst_ref=dst, send_sem=send, recv_sem=recv, device_id=device, device_id_type=MESH
        )

    def z_peer(zz):
        return (me_l, yh * 8 + zz)

    def x_peer(i):
        return ((yl * 8 + lax.rem(x + i, 8)) * 2 + core, me_h)

    def y_peer(i):
        return ((lax.rem(yl + i, 4) * 8 + x) * 2 + core, me_h)

    partner = (me_l, (1 - yh) * 8 + z)

    load0 = pltpu.make_async_copy(x_ref.at[:, pl.ds(64, 128)], xs.at[:, pl.ds(0, 128)], load_sem.at[0])
    load1 = pltpu.make_async_copy(x_ref.at[:, pl.ds(192, 64)], xs.at[:, pl.ds(128, 64)], load_sem.at[1])
    load_a = pltpu.make_async_copy(at_ref, at, load_sem.at[2])
    load_w = pltpu.make_async_copy(w_ref, wt_ref, load_sem.at[3])
    load_b = pltpu.make_async_copy(b_ref, bias_ref, load_sem.at[4])
    load_c = pltpu.make_async_copy(c_ref, cnt_ref, load_sem.at[5])
    own_w = pltpu.make_async_copy(w_ref, wgat.at[z], own_sem)
    for copy in (load_a, load_w, load0, load_b, load_c, load1, own_w):
        copy.start()

    barrier = pltpu.get_barrier_semaphore()
    peers = [z_peer(lax.rem(z + i, 8)) for i in range(1, 8)]
    peers += [(near, yh * 8 + zz) for near in (after, before) for zz in range(8)]
    peers += [x_peer(i) for i in range(1, 8)] + [y_peer(i) for i in range(1, 4)] + [partner]
    for peer in peers:
        pl.semaphore_signal(barrier, inc=1, device_id=peer, device_id_type=MESH)
    pl.semaphore_wait(barrier, len(peers))

    def group(i):
        return 4 * lax.rem(1 - yh + i, 2)

    halo = [
        remote(
            x_ref.at[pl.ds(group(i), 4), pl.ds(0, 64)], xs.at[pl.ds(group(i), 4), pl.ds(192, 64)],
            halo_s.at[i], halo_r.at[i], (before, me_h),
        )
        for i in range(2)
    ]
    a_halo = remote(a_ref.at[:, pl.ds(0, 64)], ah, ahalo_s, ahalo_r, (before, me_h))
    halo[0].start()
    halo[1].start()

    def up(k):
        slot = lax.rem(z + 8 - k, 8)
        src = w_ref.at[mine] if k == 0 else wgat.at[slot, mine]
        return remote(src, wgat.at[slot, mine], up_s.at[k], up_r.at[k], z_peer(lax.rem(z + 1, 8)))

    def down(k):
        slot = lax.rem(z + k, 8)
        src = w_ref.at[mine] if k == 0 else wgat.at[slot, mine]
        return remote(src, wgat.at[slot, mine], down_s.at[k], down_r.at[k], z_peer(lax.rem(z + 7, 8)))

    def to_pair(n, slot):
        return remote(wgat.at[slot, mine], wgat.at[slot, mine], pair_s.at[n], pair_r.at[n], pair)

    def to_sibling(n, slot, part):
        return remote(wgat.at[slot, part], wgat.at[slot, part], sib_s.at[n], sib_r.at[n], (sibling, me_h))

    up(0).start()
    down(0).start()

    def pump(k):
        slot = lax.rem(z + 7 - k, 8)
        up(k).wait_recv()
        if k < 3:
            up(k + 1).start()
        to_pair(k, slot).start()
        to_sibling(k, slot, mine).start()
        if k < 3:
            slot = lax.rem(z + 1 + k, 8)
            down(k).wait_recv()
            if k < 2:
                down(k + 1).start()
            to_pair(4 + k, slot).start()
            to_sibling(4 + k, slot, mine).start()

    def pass_on(k):
        slot = lax.rem(z + 7 - k, 8)
        to_pair(k, slot).wait_recv()
        to_sibling(7 + k, slot, theirs).start()
        if k < 3:
            slot = lax.rem(z + 1 + k, 8)
            to_pair(4 + k, slot).wait_recv()
            to_sibling(11 + k, slot, theirs).start()

    load_a.wait()
    for r in range(ROWS):
        a_ref[r] = at[:, r * 256:(r + 1) * 256].T
    a_halo.start()
    load_b.wait()
    biast[...] = bias_ref[...].T

    def project(c, base):
        w = wt_ref[...].reshape(192, D)
        for j in range(0, 4, 2):
            rows = xs[pl.ds(base + j, 2), c * 128:(c + 1) * 128, :].reshape(256, D)
            proj[pl.ds(base + j, 2), c * 128:(c + 1) * 128, :] = (
                dot(rows, w, NT).astype(BF16).reshape(2, 128, 192)
            )

    def window(c, r):
        p = proj[r, c * 128:(c + 1) * 128, :]
        q, k, v = p[:, 0:64], p[:, 64:128], p[:, 128:192]
        if c == 0:
            a = a_ref[r, 64:192, :]
        else:
            a = jnp.concatenate([a_ref[r, 192:256, :], ah[r]], axis=0)
        scores = dot(k, q, NT) * SCALE + biast[...]
        position = lax.broadcasted_iota(jnp.int32, (WIN, WIN), 0)
        scores = jnp.where(position < cnt_ref[2 * r + c], scores, -jnp.inf)
        top = jnp.max(scores, axis=0, keepdims=True)
        weights = jnp.exp(scores - top)
        probs = weights / jnp.sum(weights, axis=0, keepdims=True)
        grad_probs = dot(v, a, NT)
        grads = probs * (grad_probs - jnp.sum(probs * grad_probs, axis=0, keepdims=True))
        probs_low = probs.astype(BF16)
        grads_low = grads.astype(BF16)
        dv = dot(probs_low, a, NN).astype(BF16)
        dk = dot(grads_low, q, NN) * SCALE
        dq = dot(grads_low, k, TN) * SCALE
        qk = jnp.concatenate([dq, dk], axis=1).astype(BF16)
        gpf[r, c * 128:(c + 1) * 128, 0:128] = qk
        gpf[r, c * 128:(c + 1) * 128, 128:192] = dv
        for half in range(2):
            lo = half * 64
            gps[r, 2 * c + half, 0:64, :] = qk[lo:lo + 64]
            gps[r, 2 * c + half, 64:96, :] = jnp.concatenate([dv[lo:lo + 32], dv[lo + 32:lo + 64]], axis=1)

    def piece(r, n):
        block = lax.rem(2 * r + (1 if n in (1, 2) else 0), 8)
        half = 1 if n in (0, 2) else 0
        src = gps.at[r, n]
        dst = gat.at[lax.div(r, 4), half, z]
        recv = piece_r.at[lax.div(r, 4), half, z]
        lon = after if n == 3 else me_l
        far = remote(src, dst, piece_s.at[r, n], recv, (lon, yh * 8 + block))
        near = None if n == 3 else pltpu.make_async_copy(src, dst, recv)
        return block, far, near

    def send_piece(r, n):
        block, far, near = piece(r, n)
        if near is None:
            far.start()
            return

        @pl.when(block == z)
        def _():
            near.start()

        @pl.when(block != z)
        def _():
            far.start()

    def attend(c, base):
        for j in range(4):
            window(c, base + j)

    def send_group(base, pieces):
        for j in range(4):
            for n in pieces:
                send_piece(base + j, n)

    def weight_part(c):
        g = gpf[:, c * 128:(c + 1) * 128, :].reshape(1024, 192)
        for n in range(4):
            rows = xs[:, c * 128:(c + 1) * 128, n * 256:(n + 1) * 256].reshape(1024, 256)
            part = dot(g, rows, TN).reshape(2, 96, 256)
            if c == 0:
                wacc[:, :, n * 256:(n + 1) * 256] = part
            else:
                wacc[:, :, n * 256:(n + 1) * 256] += part

    load_w.wait()
    load_c.wait()
    load0.wait()
    project(0, group(0))
    attend(0, group(0))
    send_group(group(0), (0, 1))
    pump(0)
    project(0, group(1))
    attend(0, group(1))
    weight_part(0)
    load1.wait()
    a_halo.wait_recv()
    halo[0].wait_recv()
    project(1, group(0))
    pump(1)
    attend(1, group(0))
    send_group(group(0), (2, 3))
    pass_on(0)
    halo[1].wait_recv()
    project(1, group(1))
    pump(2)
    attend(1, group(1))
    weight_part(1)

    s_s[...] = wacc[1 - core].astype(BF16)
    rss = remote(s_s, r_s, rss_s, rss_r, (sibling, me_h))
    rss.start()
    pass_on(1)
    pump(3)
    send_group(group(1), range(4))
    rss.wait_recv()
    for i in range(8):
        cols = slice(i * 128, (i + 1) * 128)
        chunk = wacc[core, :, cols] + r_s[:, cols].astype(F32)
        t_x[i] = chunk
        s_x[i] = chunk.astype(BF16)
    rsx = [
        remote(s_x.at[lax.rem(x + i, 8)], r_x.at[i - 1], rsx_s.at[i - 1], rsx_r.at[i - 1], x_peer(i))
        for i in range(1, 8)
    ]
    for copy in rsx:
        copy.start()
    pass_on(2)
    pass_on(3)
    for copy in rsx:
        copy.wait_recv()
    total = t_x[x]
    for i in range(7):
        total += r_x[i].astype(F32)
    r_y[yl] = total.astype(BF16)
    rsy = [
        remote(r_y.at[yl], r_y.at[yl], rsy_s.at[i - 1], rsy_r.at[i - 1], y_peer(i)) for i in range(1, 4)
    ]
    for copy in rsy:
        copy.start()

    own_w.wait()
    for n in range(14):
        to_sibling(n, 0, 0).wait_recv()

    def gather(q):
        for half in range(2):
            for s in range(8):
                pltpu.make_async_copy(gps.at[0, 0], gat.at[q, half, s], piece_r.at[q, half, s]).wait()
        for s in range(8):
            for half in range(2):
                lo = half * 64
                lhs[s, lo:lo + 64, 0:128] = gat[q, half, s, 0:64, :]
                lhs[s, lo:lo + 32, 128:192] = gat[q, half, s, 64:96, 0:64]
                lhs[s, lo + 32:lo + 64, 128:192] = gat[q, half, s, 64:96, 64:128]

    def multiply(n):
        cols = slice(n * 256, (n + 1) * 256)
        total = None
        for s in range(8):
            part = dot(lhs[s], wgat[s, :, :, cols].reshape(192, 256), NN)
            total = part if total is None else total + part
        return total

    gather(1 - yh)
    exchange = [remote(ysend.at[n], yrecv.at[n], y_s.at[n], y_r.at[n], partner) for n in range(4)]
    for n in range(4):
        ysend[n] = multiply(n).astype(BF16)
        exchange[n].start()

    for copy in rsy:
        copy.wait_recv()
    total = r_y[0].astype(F32)
    for i in range(1, 4):
        total += r_y[i].astype(F32)
    og[core, x] = (total * WG_SCALE).astype(BF16)
    own = og.at[core, x]
    agx = [remote(own, own, agx_s.at[i - 1], agx_r.at[i - 1], x_peer(i)) for i in range(1, 8)]
    for copy in agx:
        copy.start()

    def share(i):
        part = og.at[core, lax.rem(x + 8 - i, 8)]
        return remote(part, part, ags_s.at[i], ags_r.at[i], (sibling, me_h))

    share(0).start()

    gather(yh)
    for n in range(4):
        acc[:, n * 256:(n + 1) * 256] = multiply(n)

    for i in range(1, 8):
        agx[i - 1].wait_recv()
        share(i).start()
    for n in range(4):
        cols = slice(n * 256, (n + 1) * 256)
        exchange[n].wait_recv()
        out_ref[:, cols] = (acc[:, cols] + yrecv[n].astype(F32)).astype(BF16)
    for i in range(8):
        share(i).wait_recv()
    for c in range(2):
        for i in range(8):
            wg_ref[c * 96:(c + 1) * 96, i * 128:(i + 1) * 128] = og[c, i].astype(F32)

    for k in range(4):
        up(k).wait_send()
    for k in range(3):
        down(k).wait_send()
    for n in range(7):
        to_pair(n, 0).wait_send()
    for n in range(14):
        to_sibling(n, 0, 0).wait_send()
    for i in range(8):
        share(i).wait_send()
    a_halo.wait_send()
    for copy in halo:
        copy.wait_send()

    @pl.loop(0, ROWS)
    def _(r):
        for n in range(4):
            block, far, near = piece(r, n)
            if near is None:
                far.wait_send()
            else:

                @pl.when(block != z)
                def _():
                    far.wait_send()

    for copy in [rss] + exchange + rsx + rsy + agx:
        copy.wait_send()


def shards(activations, qkv_weight, attn_grad, pos_bias, key_counts):
    dma = pltpu.SemaphoreType.DMA
    vmem = pl.BlockSpec(memory_space=pltpu.VMEM)
    hbm = pl.BlockSpec(memory_space=pltpu.MemorySpace.HBM)
    out, wg = pl.pallas_call(
        kernel,
        out_shape=(
            jax.ShapeDtypeStruct((128, D), BF16),
            jax.ShapeDtypeStruct((192, D), F32),
        ),
        in_specs=[
            hbm, hbm, hbm,
            hbm, hbm,
        ],
        out_specs=(vmem, vmem),
        scratch_shapes=[
            pltpu.VMEM((8, 256, D), BF16),
            pltpu.VMEM((4, 48, D), BF16),
            pltpu.VMEM((64, 2048), BF16),
            pltpu.VMEM((8, 256, 64), BF16),
            pltpu.VMEM((WIN, WIN), F32),
            pltpu.SMEM((16,), jnp.int32),
            pltpu.VMEM((8, 64, 64), BF16),
            pltpu.VMEM((8, 256, 192), BF16),
            pltpu.VMEM((WIN, WIN), F32),
            pltpu.VMEM((8, 256, 192), BF16),
            pltpu.VMEM((8, 4, 96, 128), BF16),
            pltpu.VMEM((2, 2, 8, 96, 128), BF16),
            pltpu.VMEM((8, 4, 48, D), BF16),
            pltpu.VMEM((8, 128, 192), BF16),
            pltpu.VMEM((128, D), F32),
            pltpu.VMEM((4, 128, 256), BF16),
            pltpu.VMEM((4, 128, 256), BF16),
            pltpu.VMEM((2, 96, D), F32),
            pltpu.VMEM((96, D), BF16),
            pltpu.VMEM((96, D), BF16),
            pltpu.VMEM((8, 96, 128), F32),
            pltpu.VMEM((8, 96, 128), BF16),
            pltpu.VMEM((7, 96, 128), BF16),
            pltpu.VMEM((4, 96, 128), BF16),
            pltpu.VMEM((2, 8, 96, 128), BF16),
            dma((6,)), dma,
            dma((2,)), dma((2,)), dma, dma,
            dma((8, 4)), dma((2, 2, 8)),
            dma((4,)), dma((4,)), dma((3,)), dma((3,)), dma((7,)), dma((7,)),
            dma((14,)), dma((14,)), dma((4,)), dma((4,)),
            dma, dma, dma((7,)), dma((7,)), dma((3,)), dma((3,)),
            dma((7,)), dma((7,)), dma((8,)), dma((8,)),
        ],
        compiler_params=pltpu.CompilerParams(
            collective_id=0, has_side_effects=True, vmem_limit_bytes=60 * 1024 * 1024
        ),
    )(
        activations.reshape(ROWS, 256, D),
        qkv_weight.T.reshape(4, 48, D),
        attn_grad.T,
        pos_bias[0],
        key_counts,
    )
    return out, wg.T


def solution(mesh):
    placed = (P("lon", None), P(None, "head"), P("lon", "head"), P("head", None, None), P("lon"))
    return jax.shard_map(
        shards,
        mesh=mesh,
        in_specs=placed,
        out_specs=(P(("lon", "head"), None), P(None, "head")),
        check_vma=False,
    )
```

```python
import math

import jax
import jax.numpy as jnp
from jax import lax
from jax.experimental import pallas as pl
from jax.experimental.pallas import tpu as pltpu
from jax.sharding import PartitionSpec as P

MESH = pl.DeviceIdType.MESH
F32 = jnp.float32
BF16 = jnp.bfloat16
D = 1024
HEAD_DIM = 64
WIN = 128
ROWS = 8
N_LON = 64
TOKENS = 131072
SCALE = 1.0 / math.sqrt(HEAD_DIM)
WG_SCALE = 1.0 / math.sqrt(TOKENS)
NT = (((1,), (1,)), ((), ()))
TN = (((0,), (0,)), ((), ()))
NN = (((1,), (0,)), ((), ()))


def dot(a, b, dims):
    return lax.dot_general(a, b, dims, preferred_element_type=F32)


def kernel(
    x_ref, w_ref, at_ref, b_ref, c_ref, out_ref, wg_ref,
    xs, wt_ref, at, a_ref, bias_ref, cnt_ref, ah, proj, biast, gpf, gps, gat, wgat, lhs, acc, ysend, yrecv,
    wacc, s_s, r_s, t_x, s_x, r_x, r_y, og,
    load_sem, own_sem, halo_s, halo_r, ahalo_s, ahalo_r, piece_s, piece_r,
    up_s, up_r, down_s, down_r, pair_s, pair_r, sib_s, sib_r, y_s, y_r,
    rss_s, rss_r, rsx_s, rsx_r, rsy_s, rsy_r, agx_s, agx_r, ags_s, ags_r,
):
    me_l = lax.axis_index("lon")
    me_h = lax.axis_index("head")
    yh, z = lax.div(me_h, 8), lax.rem(me_h, 8)
    core = lax.rem(me_l, 2)
    x = lax.rem(lax.div(me_l, 2), 8)
    yl = lax.div(me_l, 16)
    after = lax.rem(me_l + 1, N_LON)
    before = lax.rem(me_l + N_LON - 1, N_LON)
    sibling = me_l + 1 - 2 * core
    odd = lax.rem(yl, 2)
    mine, theirs = odd * 2 + core, (1 - odd) * 2 + core
    pair = (me_l + 16 - 32 * odd, me_h)

    def remote(src, dst, send, recv, device):
        return pltpu.make_async_remote_copy(
            src_ref=src, dst_ref=dst, send_sem=send, recv_sem=recv, device_id=device, device_id_type=MESH
        )

    def z_peer(zz):
        return (me_l, yh * 8 + zz)

    def x_peer(i):
        return ((yl * 8 + lax.rem(x + i, 8)) * 2 + core, me_h)

    def y_peer(i):
        return ((lax.rem(yl + i, 4) * 8 + x) * 2 + core, me_h)

    partner = (me_l, (1 - yh) * 8 + z)

    load0 = pltpu.make_async_copy(x_ref.at[:, pl.ds(64, 128)], xs.at[:, pl.ds(0, 128)], load_sem.at[0])
    load1 = pltpu.make_async_copy(x_ref.at[:, pl.ds(192, 64)], xs.at[:, pl.ds(128, 64)], load_sem.at[1])
    load_a = pltpu.make_async_copy(at_ref, at, load_sem.at[2])
    load_w = pltpu.make_async_copy(w_ref, wt_ref, load_sem.at[3])
    load_b = pltpu.make_async_copy(b_ref, bias_ref, load_sem.at[4])
    load_c = pltpu.make_async_copy(c_ref, cnt_ref, load_sem.at[5])
    own_w = pltpu.make_async_copy(w_ref, wgat.at[z], own_sem)
    for copy in (load_a, load_w, load0, load_b, load_c, load1, own_w):
        copy.start()

    barrier = pltpu.get_barrier_semaphore()
    peers = [z_peer(lax.rem(z + i, 8)) for i in range(1, 8)]
    peers += [(near, yh * 8 + zz) for near in (after, before) for zz in range(8)]
    peers += [x_peer(i) for i in range(1, 8)] + [y_peer(i) for i in range(1, 4)] + [partner]
    for peer in peers:
        pl.semaphore_signal(barrier, inc=1, device_id=peer, device_id_type=MESH)
    pl.semaphore_wait(barrier, len(peers))

    def group(i):
        return 4 * lax.rem(1 - yh + i, 2)

    halo = [
        remote(
            x_ref.at[pl.ds(group(i), 4), pl.ds(0, 64)], xs.at[pl.ds(group(i), 4), pl.ds(192, 64)],
            halo_s.at[i], halo_r.at[i], (before, me_h),
        )
        for i in range(2)
    ]
    a_halo = remote(a_ref.at[:, pl.ds(0, 64)], ah, ahalo_s, ahalo_r, (before, me_h))
    halo[0].start()
    halo[1].start()

    def up(k):
        slot = z if k < 2 else lax.rem(z + 6, 8)
        src = w_ref.at[mine] if k < 2 else wgat.at[slot, mine]
        return remote(src, wgat.at[slot, mine], up_s.at[k], up_r.at[k], z_peer(lax.rem(z + 1 + k % 2, 8)))

    def down(k):
        slot = z if k < 2 else lax.rem(z + 2, 8)
        src = w_ref.at[mine] if k < 2 else wgat.at[slot, mine]
        return remote(src, wgat.at[slot, mine], down_s.at[k], down_r.at[k], z_peer(lax.rem(z + 7 - k % 2, 8)))

    def to_pair(n, slot):
        return remote(wgat.at[slot, mine], wgat.at[slot, mine], pair_s.at[n], pair_r.at[n], pair)

    def to_sibling(n, slot, part):
        return remote(wgat.at[slot, part], wgat.at[slot, part], sib_s.at[n], sib_r.at[n], (sibling, me_h))

    for k in (1, 0):
        up(k).start()
        down(k).start()

    def pump(k):
        slot = lax.rem(z + 7 - k, 8)
        up(k).wait_recv()
        if k == 1:
            up(3).start()
            up(2).start()
        to_pair(k, slot).start()
        to_sibling(k, slot, mine).start()
        if k < 3:
            slot = lax.rem(z + 1 + k, 8)
            down(k).wait_recv()
            if k == 1:
                down(2).start()
            to_pair(4 + k, slot).start()
            to_sibling(4 + k, slot, mine).start()

    def pass_on(k):
        slot = lax.rem(z + 7 - k, 8)
        to_pair(k, slot).wait_recv()
        to_sibling(7 + k, slot, theirs).start()
        if k < 3:
            slot = lax.rem(z + 1 + k, 8)
            to_pair(4 + k, slot).wait_recv()
            to_sibling(11 + k, slot, theirs).start()

    load_a.wait()
    for r in range(ROWS):
        a_ref[r] = at[:, r * 256:(r + 1) * 256].T
    a_halo.start()
    load_b.wait()
    biast[...] = bias_ref[...].T

    def project(c, base):
        w = wt_ref[...].reshape(192, D)
        for j in range(0, 4, 2):
            rows = xs[pl.ds(base + j, 2), c * 128:(c + 1) * 128, :].reshape(256, D)
            proj[pl.ds(base + j, 2), c * 128:(c + 1) * 128, :] = (
                dot(rows, w, NT).astype(BF16).reshape(2, 128, 192)
            )

    def window(c, r):
        p = proj[r, c * 128:(c + 1) * 128, :]
        q, k, v = p[:, 0:64], p[:, 64:128], p[:, 128:192]
        if c == 0:
            a = a_ref[r, 64:192, :]
        else:
            a = jnp.concatenate([a_ref[r, 192:256, :], ah[r]], axis=0)
        scores = dot(k, q, NT) * SCALE + biast[...]
        position = lax.broadcasted_iota(jnp.int32, (WIN, WIN), 0)
        scores = jnp.where(position < cnt_ref[2 * r + c], scores, -jnp.inf)
        top = jnp.max(scores, axis=0, keepdims=True)
        weights = jnp.exp(scores - top)
        probs = weights / jnp.sum(weights, axis=0, keepdims=True)
        grad_probs = dot(v, a, NT)
        grads = probs * (grad_probs - jnp.sum(probs * grad_probs, axis=0, keepdims=True))
        probs_low = probs.astype(BF16)
        grads_low = grads.astype(BF16)
        dv = dot(probs_low, a, NN).astype(BF16)
        dk = dot(grads_low, q, NN) * SCALE
        dq = dot(grads_low, k, TN) * SCALE
        qk = jnp.concatenate([dq, dk], axis=1).astype(BF16)
        gpf[r, c * 128:(c + 1) * 128, 0:128] = qk
        gpf[r, c * 128:(c + 1) * 128, 128:192] = dv
        for half in range(2):
            lo = half * 64
            gps[r, 2 * c + half, 0:64, :] = qk[lo:lo + 64]
            gps[r, 2 * c + half, 64:96, :] = jnp.concatenate([dv[lo:lo + 32], dv[lo + 32:lo + 64]], axis=1)

    def piece(r, n):
        block = lax.rem(2 * r + (1 if n in (1, 2) else 0), 8)
        half = 1 if n in (0, 2) else 0
        src = gps.at[r, n]
        dst = gat.at[lax.div(r, 4), half, z]
        recv = piece_r.at[lax.div(r, 4), half, z]
        lon = after if n == 3 else me_l
        far = remote(src, dst, piece_s.at[r, n], recv, (lon, yh * 8 + block))
        near = None if n == 3 else pltpu.make_async_copy(src, dst, recv)
        return block, far, near

    def send_piece(r, n):
        block, far, near = piece(r, n)
        if near is None:
            far.start()
            return

        @pl.when(block == z)
        def _():
            near.start()

        @pl.when(block != z)
        def _():
            far.start()

    def attend(c, base):
        for j in range(4):
            window(c, base + j)

    def send_group(base, pieces):
        for j in range(4):
            for n in pieces:
                send_piece(base + j, n)

    def weight_part(c):
        g = gpf[:, c * 128:(c + 1) * 128, :].reshape(1024, 192)
        for n in range(4):
            rows = xs[:, c * 128:(c + 1) * 128, n * 256:(n + 1) * 256].reshape(1024, 256)
            part = dot(g, rows, TN).reshape(2, 96, 256)
            if c == 0:
                wacc[:, :, n * 256:(n + 1) * 256] = part
            else:
                wacc[:, :, n * 256:(n + 1) * 256] += part

    load_w.wait()
    load_c.wait()
    load0.wait()
    project(0, group(0))
    attend(0, group(0))
    send_group(group(0), (0, 1))
    project(0, group(1))
    attend(0, group(1))
    weight_part(0)
    pump(0)
    load1.wait()
    a_halo.wait_recv()
    halo[0].wait_recv()
    project(1, group(0))
    pump(1)
    attend(1, group(0))
    send_group(group(0), (2, 3))
    pass_on(0)
    halo[1].wait_recv()
    project(1, group(1))
    attend(1, group(1))
    weight_part(1)

    s_s[...] = wacc[1 - core].astype(BF16)
    rss = remote(s_s, r_s, rss_s, rss_r, (sibling, me_h))
    rss.start()
    pass_on(1)
    pump(2)
    pump(3)
    send_group(group(1), range(4))
    rss.wait_recv()
    for i in range(8):
        cols = slice(i * 128, (i + 1) * 128)
        chunk = wacc[core, :, cols] + r_s[:, cols].astype(F32)
        t_x[i] = chunk
        s_x[i] = chunk.astype(BF16)
    rsx = [
        remote(s_x.at[lax.rem(x + i, 8)], r_x.at[i - 1], rsx_s.at[i - 1], rsx_r.at[i - 1], x_peer(i))
        for i in range(1, 8)
    ]
    for copy in rsx:
        copy.start()
    pass_on(2)
    pass_on(3)
    for copy in rsx:
        copy.wait_recv()
    total = t_x[x]
    for i in range(7):
        total += r_x[i].astype(F32)
    r_y[yl] = total.astype(BF16)
    rsy = [
        remote(r_y.at[yl], r_y.at[yl], rsy_s.at[i - 1], rsy_r.at[i - 1], y_peer(i)) for i in range(1, 4)
    ]
    for copy in rsy:
        copy.start()

    own_w.wait()
    for n in range(14):
        to_sibling(n, 0, 0).wait_recv()

    def gather(q):
        for half in range(2):
            for s in range(8):
                pltpu.make_async_copy(gps.at[0, 0], gat.at[q, half, s], piece_r.at[q, half, s]).wait()
        for s in range(8):
            for half in range(2):
                lo = half * 64
                lhs[s, lo:lo + 64, 0:128] = gat[q, half, s, 0:64, :]
                lhs[s, lo:lo + 32, 128:192] = gat[q, half, s, 64:96, 0:64]
                lhs[s, lo + 32:lo + 64, 128:192] = gat[q, half, s, 64:96, 64:128]

    def multiply(n):
        cols = slice(n * 256, (n + 1) * 256)
        total = None
        for s in range(8):
            part = dot(lhs[s], wgat[s, :, :, cols].reshape(192, 256), NN)
            total = part if total is None else total + part
        return total

    gather(1 - yh)
    exchange = [remote(ysend.at[n], yrecv.at[n], y_s.at[n], y_r.at[n], partner) for n in range(4)]
    for n in range(4):
        ysend[n] = multiply(n).astype(BF16)
        exchange[n].start()

    for copy in rsy:
        copy.wait_recv()
    total = r_y[0].astype(F32)
    for i in range(1, 4):
        total += r_y[i].astype(F32)
    og[core, x] = (total * WG_SCALE).astype(BF16)
    own = og.at[core, x]
    agx = [remote(own, own, agx_s.at[i - 1], agx_r.at[i - 1], x_peer(i)) for i in range(1, 8)]
    for copy in agx:
        copy.start()

    def share(i):
        part = og.at[core, lax.rem(x + 8 - i, 8)]
        return remote(part, part, ags_s.at[i], ags_r.at[i], (sibling, me_h))

    share(0).start()

    gather(yh)
    for n in range(4):
        acc[:, n * 256:(n + 1) * 256] = multiply(n)

    for i in range(1, 8):
        agx[i - 1].wait_recv()
        share(i).start()
    for n in range(4):
        cols = slice(n * 256, (n + 1) * 256)
        exchange[n].wait_recv()
        out_ref[:, cols] = (acc[:, cols] + yrecv[n].astype(F32)).astype(BF16)
    for i in range(8):
        share(i).wait_recv()
    wg_ref[...] = og[...]

    for k in range(4):
        up(k).wait_send()
    for k in range(3):
        down(k).wait_send()
    for n in range(7):
        to_pair(n, 0).wait_send()
    for n in range(14):
        to_sibling(n, 0, 0).wait_send()
    for i in range(8):
        share(i).wait_send()
    a_halo.wait_send()
    for copy in halo:
        copy.wait_send()

    @pl.loop(0, ROWS)
    def _(r):
        for n in range(4):
            block, far, near = piece(r, n)
            if near is None:
                far.wait_send()
            else:

                @pl.when(block != z)
                def _():
                    far.wait_send()

    for copy in [rss] + exchange + rsx + rsy + agx:
        copy.wait_send()


def finish(part_ref, og_ref, out_ref, wg_ref):
    out_ref[...] = part_ref[...]
    for c in range(2):
        for i in range(8):
            wg_ref[c * 96:(c + 1) * 96, i * 128:(i + 1) * 128] = og_ref[c, i].astype(F32)


def shards(activations, qkv_weight, attn_grad, pos_bias, key_counts):
    dma = pltpu.SemaphoreType.DMA
    vmem = pl.BlockSpec(memory_space=pltpu.VMEM)
    hbm = pl.BlockSpec(memory_space=pltpu.MemorySpace.HBM)
    out, wg = pl.pallas_call(
        kernel,
        out_shape=(
            jax.ShapeDtypeStruct((128, D), BF16),
            jax.ShapeDtypeStruct((2, 8, 96, 128), BF16),
        ),
        in_specs=[
            hbm, hbm, hbm,
            hbm, hbm,
        ],
        out_specs=(vmem, vmem),
        scratch_shapes=[
            pltpu.VMEM((8, 256, D), BF16),
            pltpu.VMEM((4, 48, D), BF16),
            pltpu.VMEM((64, 2048), BF16),
            pltpu.VMEM((8, 256, 64), BF16),
            pltpu.VMEM((WIN, WIN), F32),
            pltpu.SMEM((16,), jnp.int32),
            pltpu.VMEM((8, 64, 64), BF16),
            pltpu.VMEM((8, 256, 192), BF16),
            pltpu.VMEM((WIN, WIN), F32),
            pltpu.VMEM((8, 256, 192), BF16),
            pltpu.VMEM((8, 4, 96, 128), BF16),
            pltpu.VMEM((2, 2, 8, 96, 128), BF16),
            pltpu.VMEM((8, 4, 48, D), BF16),
            pltpu.VMEM((8, 128, 192), BF16),
            pltpu.VMEM((128, D), F32),
            pltpu.VMEM((4, 128, 256), BF16),
            pltpu.VMEM((4, 128, 256), BF16),
            pltpu.VMEM((2, 96, D), F32),
            pltpu.VMEM((96, D), BF16),
            pltpu.VMEM((96, D), BF16),
            pltpu.VMEM((8, 96, 128), F32),
            pltpu.VMEM((8, 96, 128), BF16),
            pltpu.VMEM((7, 96, 128), BF16),
            pltpu.VMEM((4, 96, 128), BF16),
            pltpu.VMEM((2, 8, 96, 128), BF16),
            dma((6,)), dma,
            dma((2,)), dma((2,)), dma, dma,
            dma((8, 4)), dma((2, 2, 8)),
            dma((4,)), dma((4,)), dma((3,)), dma((3,)), dma((7,)), dma((7,)),
            dma((14,)), dma((14,)), dma((4,)), dma((4,)),
            dma, dma, dma((7,)), dma((7,)), dma((3,)), dma((3,)),
            dma((7,)), dma((7,)), dma((8,)), dma((8,)),
        ],
        compiler_params=pltpu.CompilerParams(
            collective_id=0, has_side_effects=True, vmem_limit_bytes=60 * 1024 * 1024
        ),
    )(
        activations.reshape(ROWS, 256, D),
        qkv_weight.T.reshape(4, 48, D),
        attn_grad.T,
        pos_bias[0],
        key_counts,
    )
    out, wg = pl.pallas_call(
        finish,
        out_shape=(jax.ShapeDtypeStruct((128, D), BF16), jax.ShapeDtypeStruct((192, D), F32)),
        in_specs=[vmem, vmem],
        out_specs=(vmem, vmem),
        compiler_params=pltpu.CompilerParams(vmem_limit_bytes=60 * 1024 * 1024),
    )(out, wg)
    return out, wg.T


def solution(mesh):
    placed = (P("lon", None), P(None, "head"), P("lon", "head"), P("head", None, None), P("lon"))
    return jax.shard_map(
        shards,
        mesh=mesh,
        in_specs=placed,
        out_specs=(P(("lon", "head"), None), P(None, "head")),
        check_vma=False,
    )
```
